32 devices in a mesh: face: 4 (over z), tile: 8 (over y, x, core).
Axes of the slice: x: 2, y: 2, z: 4, core: 2. Of those that a mesh axis runs over, the one named last changes fastest.
Arguments:
- sensitivity: float32 [8, 4, 512, 1536], P(None, None, ('face', 'tile')), may hold values from -6 to 6
- west_weight: float32 [8, 512, 1536], P(None, ('face', 'tile')), may hold values from 0.02 to 0.45
- east_weight: float32 [8, 512, 1536], P(None, ('face', 'tile')), may hold values from 0.02 to 0.45
- south_weight: float32 [8, 512, 1536], P(None, ('face', 'tile')), may hold values from 0.02 to 0.45
- north_weight: float32 [8, 512, 1536], P(None, ('face', 'tile')), may hold values from 0.02 to 0.45
- mixing_rate: float32 [7, 512, 1536], P(None, ('face', 'tile')), may hold values from 0.1 to 10
- extents: int32 [4, 8], replicated, may hold values from 1 to 16, 96 in all within a row
- rotation: int32 [4, 8], replicated, may hold values from 0 to 1
- regrid_weight: bfloat16 [3072, 256, 128], P(('face', 'tile')), may hold values from -0.375 to 0.375
- owner: int32 [3072, 1], P(('face', 'tile')), may hold values from 0 to 31; in each aligned block of 96 rows (0 to 95, 96 to 191, ...) at most 6 rows name the same one
- inv_slot: int32 [3072], P(('face', 'tile')), may hold values from 0 to 7
Outputs:
- adjoint_start: float32 [8, 4, 512, 1536], P(None, None, ('face', 'tile'))
- emission_grad: float32 [256, 4, 128], P(('face', 'tile'))
The draws below stay inside these ranges and needn't reach their ends.
Inputs may be any that keep to these rules, and one draw needn't show every extreme that they name: The 8 extents of each face sum to 96, and the largest of each face is 16. Of the 96 blocks of one tile at most 6 name the same owner, a bound that some block reaches of them.
All inputs are finite; a program needn't handle non-finite values.
Results may differ from the reference program's by a relative error of at most 0.0029.
Values sent between devices are 32-bit elements; how exact they have to be, the bound alone decides.
A program may use at most 128 MiB of HBM per device.

```python
import math
import jax
import jax.numpy as jnp
import numpy as np
from jax import lax

K = 8
S = 4
TILE_ROWS = 16
CY = 1536
RB = 256
EB = 128
NI = 8
NDEV = 32
FACE_ROWS = 96
NB = 96
CB = 6
N_FACE = 4
N_TILE = 8


def plant(values, own_key, least, high):
    shape = values.shape
    spot = [jax.random.randint(jax.random.fold_in(own_key, axis), (), 0, shape[axis]) for axis in range(len(shape))]
    values = values.at[tuple(spot)].set(least)
    longest = shape.index(max(shape))
    spot[longest] = (spot[longest] + 1) % shape[longest]
    return values.at[tuple(spot)].set(high)


def block_levels(stream_key, extent, shards, smallest, top_value):
    level, own = 1.0, jax.random.fold_in(stream_key, 6)
    for position, shards_of in shards:
        heights = jnp.exp(jax.random.uniform(jax.random.fold_in(own, position), (shards_of,), jnp.float32, smallest / len(shards), top_value / len(shards)))
        level = level * jnp.repeat(heights, extent[position] // shards_of).reshape([-1 if axis == position else 1 for axis in range(len(extent))])
    return level


def length_profile(count, total, most, skew):
    weights = [(1 << 20) // math.isqrt(standing ** skew) + 1 for standing in range(2, count + 1)]
    surplus, given = total - most - (count - 1), [1] * (count - 1)
    while surplus > 0:
        free = [i for i in range(count - 1) if given[i] < most]
        pool, budget = sum([weights[i] for i in free]), surplus
        for i in free:
            extra = min(most - given[i], max(1, budget * weights[i] // pool), surplus)
            given[i] = given[i] + extra
            surplus = surplus - extra
    return np.array([most] + given)


def ragged_sizes(rng, amount, total, bound, lean):
    if amount == 2:
        one = jax.random.randint(rng, (), max(1, total - bound), min(bound, total - 1) + 1)
        return jnp.stack([one, total - one])
    lengths = jnp.asarray(length_profile(amount, total, bound, lean), jnp.int32)
    pairs = (amount - 1) // 2
    source_of, sink = lengths[1:1 + 2 * pairs:2], lengths[2:2 + 2 * pairs:2]
    room = jnp.minimum(source_of - 1, bound - sink)
    passed = jax.random.randint(jax.random.fold_in(rng, 1), (pairs,), 0, 1 << 20) % (room + 1)
    lengths = lengths.at[1:1 + 2 * pairs:2].set(source_of - passed).at[2:2 + 2 * pairs:2].set(sink + passed)
    return lengths[jax.random.permutation(jax.random.fold_in(rng, 2), amount)]


def assign_block(stream_key, own, number, rows, count, top, bound, slope):
    sequence = jax.random.permutation(stream_key, count)
    crowded, ordinary = portions_of(count, rows * top, bound, slope, True), portions_of(count, rows * top, bound, slope, False)
    places = jnp.arange(count)

    def named(sizes, offset_by):
        used = int((sizes > 0).sum())
        fixed = max(1, used // 4)
        moved = fixed + (places - fixed + offset_by * (used - fixed)) % max(1, count - fixed)
        return jnp.zeros((count,), jnp.int32).at[sequence[jnp.where(places < fixed, places, moved)]].set(jnp.asarray(sizes, jnp.int32))

    sizes = jnp.where(number % 4 == 0, named(crowded, number // 4), named(ordinary, number - number // 4 - 1))
    mixed = jax.random.permutation(jax.random.fold_in(own, 3), count)
    source_of, taker = mixed[0:count // 2 * 2:2], mixed[1:count // 2 * 2:2]
    slack = jnp.minimum(sizes[source_of] - 1, bound - sizes[taker]) // 2
    slack = jnp.where((source_of == sequence[0]) | (taker == sequence[0]) | (sizes[taker] == 0), 0, jnp.maximum(slack, 0))
    moved = jax.random.randint(jax.random.fold_in(own, 4), (count // 2,), 0, 1 << 20) % (slack + 1)
    sizes = sizes.at[source_of].add(-moved).at[taker].add(moved)
    members = jnp.searchsorted(jnp.cumsum(sizes), jnp.arange(rows * top), side="right").astype(jnp.int32)
    table = members.reshape(top, rows).T
    table = table[jax.random.permutation(jax.random.fold_in(own, 1), rows)]
    offset_by = jax.random.randint(jax.random.fold_in(own, 2), (rows, 1), 0, top)
    return jnp.take_along_axis(table, (jnp.arange(top)[None, :] + offset_by) % top, axis=1)


def portions_of(number_of, total, limit, lean, full):
    portions = [(1 << 20) // math.isqrt(standing ** lean) + 1 for standing in range(1, number_of + 1)]
    largest = limit if full else min(limit, max(-(-total // number_of), total * portions[0] // sum(portions)))
    least = 1 if total - largest >= number_of - 1 else 0
    counts, rest = [largest] + [least] * (number_of - 1), total - largest - least * (number_of - 1)
    while rest > 0:
        free = [i for i in range(1, number_of) if counts[i] < largest] or [i for i in range(1, number_of) if counts[i] < limit]
        whole, budget = sum([portions[i] for i in free]), rest
        for i in free:
            extra = min(limit - counts[i], max(1, budget * portions[i] // whole), rest)
            counts[i] = counts[i] + extra
            rest = rest - extra
    return np.array(counts)


def scatter_about(key, dims, deviation, limit, cuts=(), kind=jnp.bfloat16):
    values = deviation * jax.random.normal(key, dims, jnp.float32)
    if cuts:
        values = values * block_levels(key, dims, cuts, -0.22, 0.18)
    return jnp.clip(values, -limit, limit).astype(kind)


def setup_inputs(seed: int = 0) -> dict:
    arg_keys = jax.random.split(jax.random.key(seed), 12)
    sensitivity = scatter_about(arg_keys[0], (K, S, NDEV * TILE_ROWS, CY), 1.0, 6.0, ((2, 32),), jnp.float32)
    west_weight = jnp.clip(0.02 + 0.42999999 * jax.random.uniform(arg_keys[1], (K, NDEV * TILE_ROWS, CY), jnp.float32) ** block_levels(arg_keys[1], (K, NDEV * TILE_ROWS, CY), ((1, 32),), -0.2, 0.2), 0.02, 0.45)
    east_weight = jnp.clip(0.02 + 0.42999999 * jax.random.uniform(arg_keys[2], (K, NDEV * TILE_ROWS, CY), jnp.float32) ** block_levels(arg_keys[2], (K, NDEV * TILE_ROWS, CY), ((1, 32),), -0.2, 0.2), 0.02, 0.45)
    south_weight = jnp.clip(0.02 + 0.42999999 * jax.random.uniform(arg_keys[3], (K, NDEV * TILE_ROWS, CY), jnp.float32) ** block_levels(arg_keys[3], (K, NDEV * TILE_ROWS, CY), ((1, 32),), -0.2, 0.2), 0.02, 0.45)
    north_weight = jnp.clip(0.02 + 0.42999999 * jax.random.uniform(arg_keys[4], (K, NDEV * TILE_ROWS, CY), jnp.float32) ** block_levels(arg_keys[4], (K, NDEV * TILE_ROWS, CY), ((1, 32),), -0.2, 0.2), 0.02, 0.45)
    mixing_rate = jnp.clip(jnp.exp(math.log(10.0) - 4.6051702 * jax.random.uniform(arg_keys[5], (K - 1, NDEV * TILE_ROWS, CY), jnp.float32) ** block_levels(arg_keys[5], (K - 1, NDEV * TILE_ROWS, CY), ((1, 32),), -0.2, 0.2)), 0.1, 10.0)
    extents = jax.vmap(lambda own: ragged_sizes(own, N_TILE, FACE_ROWS, TILE_ROWS, 2))(jax.random.split(arg_keys[6], N_FACE)).reshape((N_FACE, N_TILE)).astype(jnp.int32)
    rotation = plant(jax.random.randint(arg_keys[7], (N_FACE, N_TILE), 0, 2), jax.random.fold_in(arg_keys[7], 1), 0, 1).astype(jnp.int32)
    regrid_weight = scatter_about(arg_keys[8], (NDEV * NB, RB, EB), RB ** -0.5, 0.375, ((0, 32),))
    owner_keys = jax.random.split(jax.random.fold_in(arg_keys[9], 1), (NDEV * NB) // NB)
    owner_turns = jax.random.permutation(jax.random.fold_in(arg_keys[9], 3), (NDEV * NB) // NB)
    owner = jax.vmap(lambda own, number: assign_block(jax.random.fold_in(arg_keys[9], 2), own, number, NB, NDEV, 1, CB, 2))(owner_keys, owner_turns).reshape((NDEV * NB, 1))
    inv_slot = plant(jax.random.randint(arg_keys[10], (NDEV * NB,), 0, NI), jax.random.fold_in(arg_keys[10], 1), 0, NI - 1).astype(jnp.int32)
    return {"sensitivity": sensitivity, "west_weight": west_weight, "east_weight": east_weight, "south_weight": south_weight, "north_weight": north_weight, "mixing_rate": mixing_rate, "extents": extents, "rotation": rotation, "regrid_weight": regrid_weight, "owner": owner, "inv_slot": inv_slot}


def meridional(adjoint, south_rate, north_rate):
    south_flux = south_rate * adjoint
    north_flux = north_rate * adjoint
    edge_zero = jnp.zeros_like(adjoint[..., :1])
    return ((1.0 - south_rate - north_rate) * adjoint
            + jnp.concatenate([south_flux[..., 1:], edge_zero], axis=-1)
            + jnp.concatenate([edge_zero, north_flux[..., :-1]], axis=-1))


def vertical_solve(rhs, rate):
    count = rhs.shape[0]
    diagonal_terms = []
    for level in range(count):
        value = 1.0 + jnp.zeros_like(rate[0])
        if level > 0:
            value = value + rate[level - 1]
        if level < count - 1:
            value = value + rate[level]
        diagonal_terms.append(value)
    pivot = diagonal_terms[0]
    upper_part = [-rate[0] / pivot]
    solved = [rhs[0] / pivot]
    for level in range(1, count):
        pivot = diagonal_terms[level] + rate[level - 1] * upper_part[-1]
        if level < count - 1:
            upper_part.append(-rate[level] / pivot)
        solved.append((rhs[level] + rate[level - 1] * solved[-1]) / pivot)
    result = [solved[-1]]
    for level in range(count - 2, -1, -1):
        result.insert(0, solved[level] - upper_part[level] * result[0])
    return jnp.stack(result)


def reference(sensitivity, west_weight, east_weight, south_weight, north_weight, mixing_rate, extents, rotation, regrid_weight, owner, inv_slot):
    device_count = N_FACE * N_TILE
    ext_all = extents.reshape(device_count)
    rot_all = rotation.reshape(device_count)
    row_ids = jnp.arange(TILE_ROWS, dtype=jnp.int32)
    ftype = sensitivity.dtype
    live_rows = (row_ids[None, :] < ext_all[:, None]).astype(ftype)[:, :, None]
    first_pick = (row_ids == 0).astype(ftype)[None, :, None]
    last_pick = (row_ids[None, :] == ext_all[:, None] - 1).astype(ftype)[:, :, None]
    shape_five = (K, 1, device_count, TILE_ROWS, CY)
    adjoint = sensitivity.reshape(K, S, device_count, TILE_ROWS, CY) * live_rows
    west_rate = west_weight.reshape(shape_five)
    east_rate = east_weight.reshape(shape_five)
    west_flux = west_rate * adjoint
    east_flux = east_rate * adjoint
    east_edge = jnp.sum(east_flux * last_pick, axis=3)
    west_edge = west_flux[:, :, :, 0, :]
    from_west = jnp.roll(east_edge, 1, axis=2)
    from_west = jnp.where(rot_all[None, None, :, None] == 1, jnp.flip(from_west, -1), from_west)
    from_east = jnp.roll(west_edge, -1, axis=2)
    rot_next = jnp.roll(rot_all, -1)
    from_east = jnp.where(rot_next[None, None, :, None] == 1, jnp.flip(from_east, -1), from_east)
    zero_row = jnp.zeros_like(adjoint[:, :, :, :1])
    moved = ((1.0 - west_rate - east_rate) * adjoint
             + jnp.concatenate([west_flux[:, :, :, 1:], zero_row], axis=3)
             + jnp.concatenate([zero_row, east_flux[:, :, :, :-1]], axis=3))
    moved = (moved + first_pick * from_west[:, :, :, None] + last_pick * from_east[:, :, :, None]) * live_rows
    moved = meridional(moved, south_weight.reshape(shape_five), north_weight.reshape(shape_five))
    rate = mixing_rate.reshape(K - 1, 1, device_count, TILE_ROWS, CY)
    adjoint_start = vertical_solve(moved, rate)
    surface = adjoint_start[0].astype(jnp.bfloat16)
    surface = jnp.transpose(surface, (1, 0, 2, 3)).reshape(device_count, S, NB, RB)
    weights = regrid_weight.reshape(device_count, NB, RB, EB)

    def one_tile(pair):
        tile_surface, tile_weight = pair
        return jnp.einsum('snr,nre->nse', tile_surface.astype(jnp.float32), tile_weight.astype(jnp.float32), precision=lax.Precision.HIGHEST)

    terms = lax.map(one_tile, (surface, weights))
    target = (owner.reshape(-1) * NI + inv_slot).astype(jnp.int32)
    grad = jax.ops.segment_sum(terms.reshape(device_count * NB, S * EB), target, num_segments=device_count * NI)
    return adjoint_start.reshape(K, S, device_count * TILE_ROWS, CY), grad.reshape(device_count * NI, S, EB)
```

```python
import functools

import jax
import jax.numpy as jnp
from jax import lax
from jax.experimental import pallas as pl
from jax.experimental.pallas import tpu as pltpu
from jax.sharding import PartitionSpec as P

NI = 8
LANES = 128
MESH = pl.DeviceIdType.MESH


def edge_kernel(faces, tiles, ext_ref, sens_hbm, west_hbm, east_hbm, from_west, from_east,
                sens_v, west_v, east_v, east_edge, west_edge, load_sem, send_sem, recv_sem):
    levels, species = sens_v.shape[:2]
    face, tile = lax.axis_index("face"), lax.axis_index("tile")
    count = faces * tiles
    position = face * tiles + tile
    after, before = lax.rem(position + 1, count), lax.rem(position + count - 1, count)
    after = (after // tiles, lax.rem(after, tiles))
    before = (before // tiles, lax.rem(before, tiles))
    barrier = pltpu.get_barrier_semaphore()
    for other in (after, before):
        pl.semaphore_signal(barrier, inc=1, device_id=other, device_id_type=MESH)
    loads = [
        pltpu.make_async_copy(source, sink, load_sem.at[number])
        for number, (source, sink) in enumerate(
            ((sens_hbm, sens_v), (west_hbm, west_v), (east_hbm, east_v))
        )
    ]
    for load in loads:
        load.start()
    for load in loads:
        load.wait()
    last = ext_ref[face, tile] - 1
    picked = lax.broadcasted_iota(jnp.int32, sens_v.shape[2:], 0) == last
    for level in range(levels):
        east_rows = jnp.where(picked, east_v[level], 0.0)
        for kind in range(species):
            row = level * species + kind
            east_edge[row:row + 1, :] = jnp.sum(
                east_rows * sens_v[level, kind], axis=0, keepdims=True)
    pl.semaphore_wait(barrier, 2)
    forward = pltpu.make_async_remote_copy(
        src_ref=east_edge, dst_ref=from_west, send_sem=send_sem.at[0], recv_sem=recv_sem.at[0],
        device_id=after, device_id_type=MESH)
    forward.start()
    for level in range(levels):
        west_row = west_v[level, 0:1, :]
        for kind in range(species):
            row = level * species + kind
            west_edge[row:row + 1, :] = west_row * sens_v[level, kind, 0:1, :]
    backward = pltpu.make_async_remote_copy(
        src_ref=west_edge, dst_ref=from_east, send_sem=send_sem.at[1], recv_sem=recv_sem.at[1],
        device_id=before, device_id_type=MESH)
    backward.start()
    forward.wait()
    backward.wait()


def tile_kernel(faces, tiles, ext_ref, rot_ref, sens_hbm, west_hbm, east_hbm, south_hbm, north_hbm,
                rate_hbm, regrid_hbm, fw_hbm, fe_hbm, target_ref, out_hbm, part_ref,
                sens_v, west_v, east_v, south_v, north_v, rate_v, regrid_v, fw_v, fe_v, fw_k, fe_k,
                solved, upper, flat, terms, level_sem, rate_sem, regrid_sem, edge_sem, out_sem):
    levels, species, rows, width = sens_v.shape
    chunks = width // LANES
    blocks, cells, inv_cells = regrid_v.shape
    per_row = width // cells
    face, tile = lax.axis_index("face"), lax.axis_index("tile")
    count = faces * tiles
    after = lax.rem(face * tiles + tile + 1, count)
    extent = ext_ref[face, tile]
    my_rotation = rot_ref[face, tile]
    next_rotation = rot_ref[after // tiles, lax.rem(after, tiles)]

    edges = [
        pltpu.make_async_copy(fw_hbm, fw_v, edge_sem.at[0]),
        pltpu.make_async_copy(fe_hbm, fe_v, edge_sem.at[1]),
    ]
    rates = pltpu.make_async_copy(rate_hbm, rate_v.at[pl.ds(1, levels - 1)], rate_sem)
    regrid = pltpu.make_async_copy(regrid_hbm, regrid_v, regrid_sem)

    def level_copies(level):
        pairs = ((sens_hbm, sens_v), (west_hbm, west_v), (east_hbm, east_v),
                 (south_hbm, south_v), (north_hbm, north_v))
        return [
            pltpu.make_async_copy(source.at[level], sink.at[level], level_sem.at[number, level])
            for number, (source, sink) in enumerate(pairs)
        ]

    for edge in edges:
        edge.start()
    for copy in level_copies(0):
        copy.start()
    rates.start()
    for level in range(1, levels):
        for copy in level_copies(level):
            copy.start()
    regrid.start()

    zero_field = jnp.zeros((rows, width), jnp.float32)
    upper[0] = zero_field
    for kind in range(species):
        solved[0, kind] = zero_field
    flat[...] = jnp.zeros_like(flat)
    for edge in edges:
        edge.wait()

    def flip(ref):
        back = (lax.broadcasted_iota(jnp.int32, (LANES, LANES), 0)
                + lax.broadcasted_iota(jnp.int32, (LANES, LANES), 1) == LANES - 1).astype(jnp.float32)
        value = [
            jnp.dot(ref[:, c * LANES:(c + 1) * LANES], back, precision=lax.Precision.HIGHEST,
                    preferred_element_type=jnp.float32)
            for c in range(chunks)
        ]
        for c in range(chunks):
            ref[:, c * LANES:(c + 1) * LANES] = value[chunks - 1 - c]

    @pl.when(my_rotation == 1)
    def _():
        flip(fw_v)

    @pl.when(next_rotation == 1)
    def _():
        flip(fe_v)

    for source, sink in ((fw_v, fw_k), (fe_v, fe_k)):
        for level in range(levels):
            sink[level] = source[level * species:(level + 1) * species, :]
    rates.wait()
    rate_v[0] = zero_field
    rate_v[levels] = zero_field
    row_ids = lax.broadcasted_iota(jnp.int32, (rows, LANES), 0)
    lane_ids = lax.broadcasted_iota(jnp.int32, (rows, LANES), 1)
    live = row_ids < extent
    first, last = row_ids == 0, row_ids == extent - 1
    lane_first, lane_last = lane_ids == 0, lane_ids == LANES - 1
    zero = jnp.zeros((rows, LANES), jnp.float32)

    def forward(level, carry):
        for copy in level_copies(level):
            copy.wait()
        held = None
        before = [zero] * species
        for c in range(chunks + 1):
            fresh = [(None, zero, zero)] * species
            if c < chunks:
                cols = slice(c * LANES, (c + 1) * LANES)
                west, east = west_v[level, :, cols], east_v[level, :, cols]
                south, north = south_v[level, :, cols], north_v[level, :, cols]
                keep_x = 1.0 - west - east
                keep_y = 1.0 - south - north
                fresh = []
                for kind in range(species):
                    adjoint = jnp.where(live, sens_v[level, kind, :, cols], 0.0)
                    up = jnp.where(last, fe_k[level, kind:kind + 1, cols], pltpu.roll(west * adjoint, rows - 1, 0))
                    down = jnp.where(first, fw_k[level, kind:kind + 1, cols], pltpu.roll(east * adjoint, 1, 0))
                    moved = jnp.where(live, keep_x * adjoint + up + down, 0.0)
                    fresh.append((
                        keep_y * moved,
                        pltpu.roll(south * moved, LANES - 1, 1),
                        pltpu.roll(north * moved, 1, 1),
                    ))
            if c > 0:
                cols = slice((c - 1) * LANES, c * LANES)
                low, high = rate_v[level, :, cols], rate_v[level + 1, :, cols]
                pivot = (1.0 + low + high) + low * upper[level, :, cols]
                inverse = 1.0 / pivot
                upper[level + 1, :, cols] = -high * inverse
                for kind in range(species):
                    centre, left, right = held[kind]
                    y_adjoint = (centre + jnp.where(lane_last, fresh[kind][1], left)
                                 + jnp.where(lane_first, before[kind], right))
                    solved[level + 1, kind, :, cols] = (
                        y_adjoint + low * solved[level, kind, :, cols]) * inverse
                before = [held[kind][2] for kind in range(species)]
            held = fresh
        return carry

    lax.fori_loop(0, levels, forward, 0)

    def out_copy(level):
        return pltpu.make_async_copy(solved.at[level + 1], out_hbm.at[level], out_sem.at[level])

    out_copy(levels - 1).start()

    def backward(step, carry):
        level = levels - 2 - step
        for c in range(chunks):
            cols = slice(c * LANES, (c + 1) * LANES)
            factor = upper[level + 1, :, cols]
            for kind in range(species):
                solved[level + 1, kind, :, cols] = (
                    solved[level + 1, kind, :, cols] - factor * solved[level + 2, kind, :, cols])
        out_copy(level).start()
        return carry

    lax.fori_loop(0, levels - 1, backward, 0)

    for c in range(chunks):
        for kind in range(species):
            flat[c, pl.ds(kind, rows, stride=8), :] = solved[1, kind, :, c * LANES:(c + 1) * LANES]
    regrid.wait()
    lane_parts = cells // LANES

    def regrid_row(row, carry):
        for part in range(per_row):
            surface = jnp.concatenate(
                [flat[part * lane_parts + p, pl.ds(pl.multiple_of(row * 8, 8), 8), :] for p in range(lane_parts)],
                axis=1).astype(jnp.bfloat16)
            block = row * per_row + part
            terms[pl.ds(pl.multiple_of(block * 8, 8), 8), :] = jnp.dot(
                surface, regrid_v[block], preferred_element_type=jnp.float32)
        return carry

    lax.fori_loop(0, rows, regrid_row, 0)
    slots = count * NI
    select = (lax.broadcasted_iota(jnp.int32, (slots, blocks), 0) == target_ref[...])
    select = select.astype(jnp.float32).astype(jnp.bfloat16)
    for kind in range(species):
        value = terms[pl.ds(kind, blocks, stride=8), :]
        high = value.astype(jnp.bfloat16)
        rest = value - high.astype(jnp.float32)
        middle = rest.astype(jnp.bfloat16)
        low = (rest - middle.astype(jnp.float32)).astype(jnp.bfloat16)
        total = sum(
            jnp.dot(select, piece, preferred_element_type=jnp.float32) for piece in (high, middle, low))
        part_ref[:, kind] = total.reshape(count, NI, inv_cells)
    for level in range(levels):
        out_copy(level).wait()


def reduce_kernel(faces, tiles, part_ref, grad_ref, in_a, sum_a, in_b, sum_b, in_c,
                  send_a, recv_a, send_b, recv_b, send_c, recv_c):
    chips = tiles // 2
    face, tile = lax.axis_index("face"), lax.axis_index("tile")
    chip, core = tile // 2, lax.rem(tile, 2)
    partner = (face, tile + 1 - 2 * core)
    chip_of = [lax.rem(chip + step, chips) for step in range(chips)]
    face_of = [lax.rem(face + step, faces) for step in range(faces)]
    others = [partner]
    others += [(face, 2 * chip_of[step] + core) for step in range(1, chips)]
    others += [(face_of[step], tile) for step in range(1, faces)]
    barrier = pltpu.get_barrier_semaphore()
    for other in others:
        pl.semaphore_signal(barrier, inc=1, device_id=other, device_id_type=MESH)
    pl.semaphore_wait(barrier, len(others))

    order = list(range(1, chips)) + [0]
    first = {}
    for step in order:
        first[step] = pltpu.make_async_remote_copy(
            src_ref=part_ref.at[1 - core, chip_of[step]], dst_ref=in_a.at[step],
            send_sem=send_a.at[step], recv_sem=recv_a.at[step],
            device_id=partner, device_id_type=MESH)
        first[step].start()
    second = {}
    for step in order:
        first[step].wait_recv()
        sum_a[step] = part_ref[core, chip_of[step]] + in_a[step]
        if step > 0:
            second[step] = pltpu.make_async_remote_copy(
                src_ref=sum_a.at[step], dst_ref=in_b.at[step - 1],
                send_sem=send_b.at[step - 1], recv_sem=recv_b.at[step - 1],
                device_id=(face, 2 * chip_of[step] + core), device_id_type=MESH)
            second[step].start()
    for step in range(1, chips):
        second[step].wait_recv()
    total = sum_a[0]
    for step in range(1, chips):
        total = total + in_b[step - 1]
    sum_b[...] = total
    third = {}
    for step in range(1, faces):
        third[step] = pltpu.make_async_remote_copy(
            src_ref=sum_b.at[face_of[step]], dst_ref=in_c.at[step - 1],
            send_sem=send_c.at[step - 1], recv_sem=recv_c.at[step - 1],
            device_id=(face_of[step], tile), device_id_type=MESH)
        third[step].start()
    for step in range(1, faces):
        third[step].wait_recv()
    result = sum_b[face]
    for step in range(1, faces):
        result = result + in_c[step - 1]
    for kind in range(result.shape[0]):
        grad_ref[:, kind, :] = result[kind]
    for copies in (first, second, third):
        for copy in copies.values():
            copy.wait_send()


def per_device(faces, tiles, sensitivity, west_weight, east_weight, south_weight, north_weight,
               mixing_rate, extents, rotation, regrid_weight, owner, inv_slot):
    levels, species, rows, width = sensitivity.shape
    blocks, cells, inv_cells = regrid_weight.shape
    count, chips = faces * tiles, tiles // 2
    f32 = jnp.float32
    hbm = pl.BlockSpec(memory_space=pl.ANY)
    vmem = pl.BlockSpec(memory_space=pltpu.VMEM)
    smem = pl.BlockSpec(memory_space=pltpu.SMEM)
    dma = pltpu.SemaphoreType.DMA
    edge = jax.ShapeDtypeStruct((levels * species, width), f32)
    from_west, from_east = pl.pallas_call(
        functools.partial(edge_kernel, faces, tiles),
        out_shape=(edge, edge),
        in_specs=[smem, hbm, hbm, hbm],
        out_specs=(vmem, vmem),
        scratch_shapes=[
            pltpu.VMEM(sensitivity.shape, f32),
            pltpu.VMEM(west_weight.shape, f32),
            pltpu.VMEM(west_weight.shape, f32),
            pltpu.VMEM(edge.shape, f32),
            pltpu.VMEM(edge.shape, f32),
            dma((3,)), dma((2,)), dma((2,)),
        ],
        compiler_params=pltpu.CompilerParams(
            collective_id=0, has_side_effects=True, vmem_limit_bytes=60 << 20),
        name="edges",
    )(extents, sensitivity, west_weight, east_weight)

    owner_ids = owner[:, 0]
    owner_tile = owner_ids % tiles
    target = ((owner_tile % 2 * chips + owner_tile // 2) * faces + owner_ids // tiles) * NI + inv_slot
    adjoint_start, part = pl.pallas_call(
        functools.partial(tile_kernel, faces, tiles),
        out_shape=(
            jax.ShapeDtypeStruct(sensitivity.shape, f32),
            jax.ShapeDtypeStruct((count, species, NI, inv_cells), f32),
        ),
        in_specs=[smem, smem] + [hbm] * 9 + [vmem],
        out_specs=(hbm, vmem),
        scratch_shapes=[
            pltpu.VMEM(sensitivity.shape, f32),
            pltpu.VMEM(west_weight.shape, f32),
            pltpu.VMEM(west_weight.shape, f32),
            pltpu.VMEM(west_weight.shape, f32),
            pltpu.VMEM(west_weight.shape, f32),
            pltpu.VMEM((levels + 1, rows, width), f32),
            pltpu.VMEM(regrid_weight.shape, regrid_weight.dtype),
            pltpu.VMEM(edge.shape, f32),
            pltpu.VMEM(edge.shape, f32),
            pltpu.VMEM((levels, species, width), f32),
            pltpu.VMEM((levels, species, width), f32),
            pltpu.VMEM((levels + 1, species, rows, width), f32),
            pltpu.VMEM((levels + 1, rows, width), f32),
            pltpu.VMEM((width // LANES, rows * 8, LANES), f32),
            pltpu.VMEM((blocks * 8, inv_cells), f32),
            dma((5, levels)), dma, dma, dma((2,)), dma((levels,)),
        ],
        compiler_params=pltpu.CompilerParams(vmem_limit_bytes=60 << 20),
        name="tile",
    )(extents, rotation, sensitivity, west_weight, east_weight, south_weight, north_weight,
      mixing_rate, regrid_weight, from_west, from_east, target[None, :])

    unit = (species, NI, inv_cells)
    grad = pl.pallas_call(
        functools.partial(reduce_kernel, faces, tiles),
        out_shape=jax.ShapeDtypeStruct((NI, species, inv_cells), f32),
        in_specs=[vmem],
        out_specs=vmem,
        scratch_shapes=[
            pltpu.VMEM((chips, faces) + unit, f32),
            pltpu.VMEM((chips, faces) + unit, f32),
            pltpu.VMEM((chips - 1, faces) + unit, f32),
            pltpu.VMEM((faces,) + unit, f32),
            pltpu.VMEM((faces - 1,) + unit, f32),
            dma((chips,)), dma((chips,)), dma((chips - 1,)), dma((chips - 1,)),
            dma((faces - 1,)), dma((faces - 1,)),
        ],
        compiler_params=pltpu.CompilerParams(
            collective_id=1, has_side_effects=True, vmem_limit_bytes=24 << 20),
        name="reduce",
    )(part.reshape((2, chips, faces) + unit))
    return adjoint_start, grad


def solution(mesh):
    faces, tiles = mesh.shape["face"], mesh.shape["tile"]
    both = ("face", "tile")
    placed = (P(None, None, both, None),) + (P(None, both, None),) * 5 + (P(), P()) + (
        P(both, None, None), P(both, None), P(both))
    return jax.shard_map(
        functools.partial(per_device, faces, tiles),
        mesh=mesh,
        in_specs=placed,
        out_specs=(P(None, None, both, None), P(both, None, None)),
        check_vma=False,
    )
```

```python
import functools

import jax
import jax.numpy as jnp
from jax import lax
from jax.experimental import pallas as pl
from jax.experimental.pallas import tpu as pltpu
from jax.sharding import PartitionSpec as P

NI = 8
LANES = 128
MESH = pl.DeviceIdType.MESH


def step_kernel(faces, tiles, ext_ref, rot_ref, sens_hbm, west_hbm, east_hbm, south_hbm, north_hbm,
                rate_hbm, regrid_hbm, owner_ref, slot_ref, solved, grad_ref,
                sens_v, west_v, east_v, south_v, north_v, rate_v, regrid_v, upper,
                east_edge, west_edge, from_west, from_east, edge, edge_south, edge_north, edge_rate, edge_upper,
                flat, terms, part_ref, in_a, sum_a, in_b, sum_b, in_c,
                level_sem, rate_sem, regrid_sem, edge_send, edge_recv,
                send_a, recv_a, send_b, recv_b, send_c, recv_c):
    levels, species, rows, width = sens_v.shape
    chunks = width // LANES
    blocks, cells, inv_cells = regrid_v.shape
    per_row = width // cells
    face, tile = lax.axis_index("face"), lax.axis_index("tile")
    count, chips = faces * tiles, tiles // 2
    position = face * tiles + tile
    after, before = lax.rem(position + 1, count), lax.rem(position + count - 1, count)
    after = (after // tiles, lax.rem(after, tiles))
    before = (before // tiles, lax.rem(before, tiles))
    chip, core = tile // 2, lax.rem(tile, 2)
    partner = (face, tile + 1 - 2 * core)
    chip_of = [lax.rem(chip + step, chips) for step in range(chips)]
    face_of = [lax.rem(face + step, faces) for step in range(faces)]
    others = [after, before, partner]
    others += [(face, 2 * chip_of[step] + core) for step in range(1, chips)]
    others += [(face_of[step], tile) for step in range(1, faces)]
    barrier = pltpu.get_barrier_semaphore()
    for other in others:
        pl.semaphore_signal(barrier, inc=1, device_id=other, device_id_type=MESH)

    def level_copies(level, pairs, base):
        return [
            pltpu.make_async_copy(source.at[level], sink.at[level], level_sem.at[base + number, level])
            for number, (source, sink) in enumerate(pairs)
        ]

    x_pairs = ((sens_hbm, sens_v), (west_hbm, west_v), (east_hbm, east_v))
    y_pairs = ((south_hbm, south_v), (north_hbm, north_v))
    rates = pltpu.make_async_copy(rate_hbm, rate_v.at[pl.ds(1, levels - 1)], rate_sem)
    regrid = pltpu.make_async_copy(regrid_hbm, regrid_v, regrid_sem)
    for level in range(levels):
        for copy in level_copies(level, x_pairs, 0):
            copy.start()
    rates.start()
    for level in range(levels):
        for copy in level_copies(level, y_pairs, 3):
            copy.start()
    regrid.start()

    extent = ext_ref[face, tile]
    row_ids = lax.broadcasted_iota(jnp.int32, (rows, LANES), 0)
    lane_ids = lax.broadcasted_iota(jnp.int32, (rows, LANES), 1)
    live = row_ids < extent
    first, last = row_ids == 0, row_ids == extent - 1
    bottom = row_ids == rows - 1
    lane_first, lane_last = lane_ids == 0, lane_ids == LANES - 1
    zero = jnp.zeros((rows, LANES), jnp.float32)
    zero_field = jnp.zeros((rows, width), jnp.float32)
    upper[0] = zero_field
    rate_v[0] = zero_field
    rate_v[levels] = zero_field
    for kind in range(species):
        solved[0, kind] = zero_field
    flat[...] = jnp.zeros_like(flat)

    def column(c):
        return slice(c * LANES, (c + 1) * LANES)

    for level in range(levels):
        for copy in level_copies(level, x_pairs, 0):
            copy.wait()
        for c in range(chunks):
            east_rows = jnp.where(last, east_v[level, :, column(c)], 0.0)
            for kind in range(species):
                row = level * species + kind
                east_edge[row:row + 1, column(c)] = jnp.sum(
                    east_rows * sens_v[level, kind, :, column(c)], axis=0, keepdims=True)
        west_row = west_v[level, 0:1, :]
        for kind in range(species):
            row = level * species + kind
            west_edge[row:row + 1, :] = west_row * sens_v[level, kind, 0:1, :]
    pl.semaphore_wait(barrier, len(others))
    exchange = [
        pltpu.make_async_remote_copy(
            src_ref=source, dst_ref=sink, send_sem=edge_send.at[number], recv_sem=edge_recv.at[number],
            device_id=other, device_id_type=MESH)
        for number, (source, sink, other) in enumerate(
            ((east_edge, from_west, after), (west_edge, from_east, before)))
    ]
    for copy in exchange:
        copy.start()

    rates.wait()
    half = lax.broadcasted_iota(jnp.int32, (8, LANES), 0) < species

    def edge_rows(value):
        tail = jnp.sum(jnp.where(last, value, 0.0), axis=0, keepdims=True)
        return jnp.where(half, jnp.broadcast_to(value[0:1], (8, LANES)), jnp.broadcast_to(tail, (8, LANES)))

    def forward(level, carry):
        for copy in level_copies(level, y_pairs, 3):
            copy.wait()
        previous = jnp.maximum(level - 1, 0)
        held = None
        behind = [zero] * species
        for c in range(chunks + 1):
            fresh = [(None, zero, zero)] * species
            if c < chunks:
                cols = column(c)
                west, east = west_v[level, :, cols], east_v[level, :, cols]
                south, north = south_v[level, :, cols], north_v[level, :, cols]
                edge_south[level, :, cols] = edge_rows(south)
                edge_north[level, :, cols] = edge_rows(north)
                keep_x = 1.0 - west - east
                keep_y = 1.0 - south - north
                fresh = []
                for kind in range(species):
                    adjoint = jnp.where(live, sens_v[level, kind, :, cols], 0.0)
                    up = jnp.where(bottom, 0.0, pltpu.roll(west * adjoint, rows - 1, 0))
                    down = jnp.where(first, 0.0, pltpu.roll(east * adjoint, 1, 0))
                    moved = jnp.where(live, keep_x * adjoint + up + down, 0.0)
                    fresh.append((
                        keep_y * moved,
                        pltpu.roll(south * moved, LANES - 1, 1),
                        pltpu.roll(north * moved, 1, 1),
                    ))
            if c > 0:
                cols = column(c - 1)
                low, high = rate_v[level, :, cols], rate_v[level + 1, :, cols]
                edge_rate[level + 1, :, cols] = edge_rows(high)
                pivot = (1.0 + low + high) + low * upper[level, :, cols]
                inverse = 1.0 / pivot
                upper[level + 1, :, cols] = -high * inverse
                for kind in range(species):
                    centre, left, right = held[kind]
                    y_adjoint = (centre + jnp.where(lane_last, fresh[kind][1], left)
                                 + jnp.where(lane_first, behind[kind], right))
                    solved[level, kind, :, cols] = (
                        y_adjoint + low * solved[previous, kind, :, cols]) * inverse
                behind = [held[kind][2] for kind in range(species)]
            held = fresh
        return carry

    lax.fori_loop(0, levels, forward, 0)

    after_rotation = rot_ref[after[0], after[1]]
    my_rotation = rot_ref[face, tile]
    back = (lax.broadcasted_iota(jnp.int32, (LANES, LANES), 0)
            + lax.broadcasted_iota(jnp.int32, (LANES, LANES), 1) == LANES - 1)
    back = back.astype(jnp.float32).astype(jnp.bfloat16)

    def pieces(value):
        high = value.astype(jnp.bfloat16)
        rest = value - high.astype(jnp.float32)
        middle = rest.astype(jnp.bfloat16)
        return high, middle, (rest - middle.astype(jnp.float32)).astype(jnp.bfloat16)

    for number, (source, rotation) in enumerate(((from_west, my_rotation), (from_east, after_rotation))):
        exchange[number].wait_recv()
        straight = jnp.concatenate([source[:, column(c)] for c in range(chunks)], axis=0)
        turned = sum(jnp.dot(piece, back, preferred_element_type=jnp.float32) for piece in pieces(straight))
        height = levels * species
        reverse = jnp.full((height, LANES), rotation, jnp.int32) == 1
        for c in range(chunks):
            mirrored = chunks - 1 - c
            value = jnp.where(reverse, turned[mirrored * height:(mirrored + 1) * height],
                              straight[c * height:(c + 1) * height])
            for level in range(levels):
                edge[level, number * species:(number + 1) * species, column(c)] = (
                    value[level * species:(level + 1) * species])

    zero_edge = jnp.zeros((8, width), jnp.float32)
    edge_rate[0] = zero_edge
    edge_upper[...] = zero_edge
    nothing = jnp.zeros((8, LANES), jnp.float32)

    def forward_edge(level, carry):
        previous = jnp.maximum(level - 1, 0)
        held, behind = None, nothing
        for c in range(chunks + 1):
            fresh = (None, nothing, nothing)
            if c < chunks:
                cols = column(c)
                south, north = edge_south[level, :, cols], edge_north[level, :, cols]
                moved = edge[level, :, cols]
                fresh = ((1.0 - south - north) * moved,
                         pltpu.roll(south * moved, LANES - 1, 1), pltpu.roll(north * moved, 1, 1))
            if c > 0:
                cols = column(c - 1)
                low, high = edge_rate[level, :, cols], edge_rate[level + 1, :, cols]
                inverse = 1.0 / ((1.0 + low + high) + low * edge_upper[:, cols])
                edge_upper[:, cols] = -high * inverse
                centre, left, right = held
                y_adjoint = (centre + jnp.where(lane_last[:8], fresh[1], left)
                             + jnp.where(lane_first[:8], behind, right))
                edge[level, :, cols] = (y_adjoint + low * edge[previous, :, cols]) * inverse
                behind = right
            held = fresh
        return carry

    lax.fori_loop(0, levels, forward_edge, 0)

    def backward(step, carry):
        level = levels - 1 - step
        later = jnp.minimum(level + 1, levels - 1)
        for c in range(chunks):
            cols = column(c)
            factor = upper[level + 1, :, cols]
            for kind in range(species):
                value = solved[level, kind, :, cols]
                value = value + jnp.where(first, edge[level, kind:kind + 1, cols], 0.0)
                value = value + jnp.where(last, edge[level, species + kind:species + kind + 1, cols], 0.0)
                solved[level, kind, :, cols] = value - factor * solved[later, kind, :, cols]
        return carry

    lax.fori_loop(0, levels, backward, 0)

    for c in range(chunks):
        for kind in range(species):
            flat[c, pl.ds(kind, rows, stride=8), :] = solved[0, kind, :, column(c)]
    regrid.wait()
    lane_parts = cells // LANES

    def regrid_row(row, carry):
        for part in range(per_row):
            surface = jnp.concatenate(
                [flat[part * lane_parts + p, pl.ds(pl.multiple_of(row * 8, 8), 8), :] for p in range(lane_parts)],
                axis=1).astype(jnp.bfloat16)
            block = row * per_row + part
            terms[pl.ds(pl.multiple_of(block * 8, 8), 8), :] = jnp.dot(
                surface, regrid_v[block], preferred_element_type=jnp.float32)
        return carry

    lax.fori_loop(0, rows, regrid_row, 0)
    target = owner_ref[...] * NI + slot_ref[...]
    select = lax.broadcasted_iota(jnp.int32, (count * NI, blocks), 0) == target
    select = select.astype(jnp.float32).astype(jnp.bfloat16)
    for kind in range(species):
        value = terms[pl.ds(kind, blocks, stride=8), :]
        total = sum(jnp.dot(select, piece, preferred_element_type=jnp.float32) for piece in pieces(value))
        for number in range(count):
            spot = (number % tiles % 2, number % tiles // 2, number // tiles, kind)
            part_ref[spot] = total[number * NI:(number + 1) * NI]

    order = list(range(1, chips)) + [0]
    first = {}
    for step in order:
        first[step] = pltpu.make_async_remote_copy(
            src_ref=part_ref.at[1 - core, chip_of[step]], dst_ref=in_a.at[step],
            send_sem=send_a.at[step], recv_sem=recv_a.at[step],
            device_id=partner, device_id_type=MESH)
        first[step].start()
    second = {}
    for step in order:
        first[step].wait_recv()
        sum_a[step] = part_ref[core, chip_of[step]] + in_a[step]
        if step > 0:
            second[step] = pltpu.make_async_remote_copy(
                src_ref=sum_a.at[step], dst_ref=in_b.at[step - 1],
                send_sem=send_b.at[step - 1], recv_sem=recv_b.at[step - 1],
                device_id=(face, 2 * chip_of[step] + core), device_id_type=MESH)
            second[step].start()
    for step in range(1, chips):
        second[step].wait_recv()
    total = sum_a[0]
    for step in range(1, chips):
        total = total + in_b[step - 1]
    sum_b[...] = total
    third = {}
    for step in range(1, faces):
        third[step] = pltpu.make_async_remote_copy(
            src_ref=sum_b.at[face_of[step]], dst_ref=in_c.at[step - 1],
            send_sem=send_c.at[step - 1], recv_sem=recv_c.at[step - 1],
            device_id=(face_of[step], tile), device_id_type=MESH)
        third[step].start()
    for step in range(1, faces):
        third[step].wait_recv()
    result = sum_b[face]
    for step in range(1, faces):
        result = result + in_c[step - 1]
    for kind in range(result.shape[0]):
        grad_ref[:, kind, :] = result[kind]
    for copies in (first, second, third):
        for copy in copies.values():
            copy.wait_send()
    for copy in exchange:
        copy.wait_send()


def per_device(faces, tiles, sensitivity, west_weight, east_weight, south_weight, north_weight,
               mixing_rate, extents, rotation, regrid_weight, owner, inv_slot):
    levels, species, rows, width = sensitivity.shape
    blocks, cells, inv_cells = regrid_weight.shape
    chips = tiles // 2
    f32 = jnp.float32
    hbm = pl.BlockSpec(memory_space=pltpu.HBM)
    vmem = pl.BlockSpec(memory_space=pltpu.VMEM)
    smem = pl.BlockSpec(memory_space=pltpu.SMEM)
    dma = pltpu.SemaphoreType.DMA
    unit = (species, NI, inv_cells)
    field, line, edge = (levels, rows, width), (levels * species, width), (levels, 2 * species, width)
    shapes = [sensitivity.shape] + [field] * 4 + [(levels + 1, rows, width)]
    scratch = [pltpu.VMEM(shape, f32) for shape in shapes]
    scratch += [pltpu.VMEM(regrid_weight.shape, regrid_weight.dtype)]
    shapes = [(levels + 1, rows, width)] + [line] * 4 + [edge] * 3
    shapes += [(levels + 1, 2 * species, width), (2 * species, width)]
    shapes += [(width // LANES, rows * 8, LANES), (blocks * 8, inv_cells)]
    shapes += [(2, chips, faces) + unit, (chips, faces) + unit, (chips, faces) + unit]
    shapes += [(chips - 1, faces) + unit, (faces,) + unit, (faces - 1,) + unit]
    scratch += [pltpu.VMEM(shape, f32) for shape in shapes]
    scratch += [dma((5, levels)), dma, dma, dma((2,)), dma((2,))]
    scratch += [dma((number,)) for number in (chips, chips, chips - 1, chips - 1, faces - 1, faces - 1)]
    return pl.pallas_call(
        functools.partial(step_kernel, faces, tiles),
        out_shape=(
            jax.ShapeDtypeStruct(sensitivity.shape, f32),
            jax.ShapeDtypeStruct((NI, species, inv_cells), f32),
        ),
        in_specs=[smem, smem] + [hbm] * 7 + [vmem, vmem],
        out_specs=(vmem, vmem),
        scratch_shapes=scratch,
        compiler_params=pltpu.CompilerParams(
            collective_id=0, has_side_effects=True, vmem_limit_bytes=44 << 20),
        name="step",
    )(extents, rotation, sensitivity, west_weight, east_weight, south_weight, north_weight,
      mixing_rate, regrid_weight, owner.reshape(1, blocks), inv_slot.reshape(1, blocks))


def solution(mesh):
    faces, tiles = mesh.shape["face"], mesh.shape["tile"]
    both = ("face", "tile")
    placed = (P(None, None, both, None),) + (P(None, both, None),) * 5 + (P(), P()) + (
        P(both, None, None), P(both, None), P(both))
    return jax.shard_map(
        functools.partial(per_device, faces, tiles),
        mesh=mesh,
        in_specs=placed,
        out_specs=(P(None, None, both, None), P(both, None, None)),
        check_vma=False,
    )
```

```python
import functools

import jax
import jax.numpy as jnp
from jax import lax
from jax.experimental import pallas as pl
from jax.experimental.pallas import tpu as pltpu
from jax.sharding import PartitionSpec as P

NI = 8
LANES = 128
MESH = pl.DeviceIdType.MESH


def step_kernel(faces, tiles, ext_ref, rot_ref, sens_hbm, west_hbm, east_hbm, south_hbm, north_hbm,
                rate_hbm, regrid_hbm, owner_ref, slot_ref, out_hbm, grad_ref,
                sens_v, west_v, east_v, south_v, north_v, rate_v, regrid_v, solved, upper,
                east_edge, west_edge, from_west, from_east, edge, edge_south, edge_north, edge_rate, edge_upper,
                flat, terms, part_ref, in_a, sum_a, in_b, sum_b, in_c,
                level_sem, rate_sem, regrid_sem, edge_send, edge_recv, out_sem,
                send_a, recv_a, send_b, recv_b, send_c, recv_c):
    levels, species, rows, width = sens_v.shape
    chunks = width // LANES
    blocks, cells, inv_cells = regrid_v.shape
    per_row = width // cells
    face, tile = lax.axis_index("face"), lax.axis_index("tile")
    count, chips = faces * tiles, tiles // 2
    position = face * tiles + tile
    after, before = lax.rem(position + 1, count), lax.rem(position + count - 1, count)
    after = (after // tiles, lax.rem(after, tiles))
    before = (before // tiles, lax.rem(before, tiles))
    chip, core = tile // 2, lax.rem(tile, 2)
    partner = (face, tile + 1 - 2 * core)
    chip_of = [lax.rem(chip + step, chips) for step in range(chips)]
    face_of = [lax.rem(face + step, faces) for step in range(faces)]
    others = [after, before, partner]
    others += [(face, 2 * chip_of[step] + core) for step in range(1, chips)]
    others += [(face_of[step], tile) for step in range(1, faces)]
    barrier = pltpu.get_barrier_semaphore()
    for other in others:
        pl.semaphore_signal(barrier, inc=1, device_id=other, device_id_type=MESH)

    def level_copies(level, pairs, base):
        return [
            pltpu.make_async_copy(source.at[level], sink.at[level], level_sem.at[base + number, level])
            for number, (source, sink) in enumerate(pairs)
        ]

    x_pairs = ((sens_hbm, sens_v), (west_hbm, west_v), (east_hbm, east_v))
    y_pairs = ((south_hbm, south_v), (north_hbm, north_v))
    rates = pltpu.make_async_copy(rate_hbm, rate_v.at[pl.ds(1, levels - 1)], rate_sem)
    regrid = pltpu.make_async_copy(regrid_hbm, regrid_v, regrid_sem)
    for level in range(levels):
        for copy in level_copies(level, x_pairs, 0):
            copy.start()
    rates.start()
    for level in range(levels):
        for copy in level_copies(level, y_pairs, 3):
            copy.start()
    regrid.start()

    extent = ext_ref[face, tile]
    row_ids = lax.broadcasted_iota(jnp.int32, (rows, LANES), 0)
    lane_ids = lax.broadcasted_iota(jnp.int32, (rows, LANES), 1)
    live = row_ids < extent
    first, last = row_ids == 0, row_ids == extent - 1
    bottom = row_ids == rows - 1
    lane_first, lane_last = lane_ids == 0, lane_ids == LANES - 1
    zero = jnp.zeros((rows, LANES), jnp.float32)
    zero_field = jnp.zeros((rows, width), jnp.float32)
    upper[0] = zero_field
    rate_v[0] = zero_field
    rate_v[levels] = zero_field
    for kind in range(species):
        solved[0, kind] = zero_field
    flat[...] = jnp.zeros_like(flat)

    def column(c):
        return slice(c * LANES, (c + 1) * LANES)

    for level in range(levels):
        for copy in level_copies(level, x_pairs, 0):
            copy.wait()
        for c in range(chunks):
            east_rows = jnp.where(last, east_v[level, :, column(c)], 0.0)
            for kind in range(species):
                row = level * species + kind
                east_edge[row:row + 1, column(c)] = jnp.sum(
                    east_rows * sens_v[level, kind, :, column(c)], axis=0, keepdims=True)
        west_row = west_v[level, 0:1, :]
        for kind in range(species):
            row = level * species + kind
            west_edge[row:row + 1, :] = west_row * sens_v[level, kind, 0:1, :]
    pl.semaphore_wait(barrier, len(others))
    exchange = [
        pltpu.make_async_remote_copy(
            src_ref=source, dst_ref=sink, send_sem=edge_send.at[number], recv_sem=edge_recv.at[number],
            device_id=other, device_id_type=MESH)
        for number, (source, sink, other) in enumerate(
            ((east_edge, from_west, after), (west_edge, from_east, before)))
    ]
    for copy in exchange:
        copy.start()

    rates.wait()
    half = lax.broadcasted_iota(jnp.int32, (8, LANES), 0) < species

    def edge_rows(value):
        tail = jnp.sum(jnp.where(last, value, 0.0), axis=0, keepdims=True)
        return jnp.where(half, jnp.broadcast_to(value[0:1], (8, LANES)), jnp.broadcast_to(tail, (8, LANES)))

    def forward(level, carry):
        for copy in level_copies(level, y_pairs, 3):
            copy.wait()
        previous = jnp.maximum(level - 1, 0)
        held = None
        behind = [zero] * species
        for c in range(chunks + 1):
            fresh = [(None, zero, zero)] * species
            if c < chunks:
                cols = column(c)
                west, east = west_v[level, :, cols], east_v[level, :, cols]
                south, north = south_v[level, :, cols], north_v[level, :, cols]
                edge_south[level, :, cols] = edge_rows(south)
                edge_north[level, :, cols] = edge_rows(north)
                keep_x = 1.0 - west - east
                keep_y = 1.0 - south - north
                fresh = []
                for kind in range(species):
                    adjoint = jnp.where(live, sens_v[level, kind, :, cols], 0.0)
                    up = jnp.where(bottom, 0.0, pltpu.roll(west * adjoint, rows - 1, 0))
                    down = jnp.where(first, 0.0, pltpu.roll(east * adjoint, 1, 0))
                    moved = jnp.where(live, keep_x * adjoint + up + down, 0.0)
                    fresh.append((
                        keep_y * moved,
                        pltpu.roll(south * moved, LANES - 1, 1),
                        pltpu.roll(north * moved, 1, 1),
                    ))
            if c > 0:
                cols = column(c - 1)
                low, high = rate_v[level, :, cols], rate_v[level + 1, :, cols]
                edge_rate[level + 1, :, cols] = edge_rows(high)
                pivot = (1.0 + low + high) + low * upper[level, :, cols]
                inverse = 1.0 / pivot
                upper[level + 1, :, cols] = -high * inverse
                for kind in range(species):
                    centre, left, right = held[kind]
                    y_adjoint = (centre + jnp.where(lane_last, fresh[kind][1], left)
                                 + jnp.where(lane_first, behind[kind], right))
                    solved[level, kind, :, cols] = (
                        y_adjoint + low * solved[previous, kind, :, cols]) * inverse
                behind = [held[kind][2] for kind in range(species)]
            held = fresh
        return carry

    lax.fori_loop(0, levels, forward, 0)

    after_rotation = rot_ref[after[0], after[1]]
    my_rotation = rot_ref[face, tile]
    back = (lax.broadcasted_iota(jnp.int32, (LANES, LANES), 0)
            + lax.broadcasted_iota(jnp.int32, (LANES, LANES), 1) == LANES - 1)
    back = back.astype(jnp.float32).astype(jnp.bfloat16)

    def pieces(value):
        high = value.astype(jnp.bfloat16)
        rest = value - high.astype(jnp.float32)
        middle = rest.astype(jnp.bfloat16)
        return high, middle, (rest - middle.astype(jnp.float32)).astype(jnp.bfloat16)

    for number, (source, rotation) in enumerate(((from_west, my_rotation), (from_east, after_rotation))):
        exchange[number].wait_recv()
        straight = jnp.concatenate([source[:, column(c)] for c in range(chunks)], axis=0)
        turned = sum(jnp.dot(piece, back, preferred_element_type=jnp.float32) for piece in pieces(straight))
        height = levels * species
        reverse = jnp.full((height, LANES), rotation, jnp.int32) == 1
        for c in range(chunks):
            mirrored = chunks - 1 - c
            value = jnp.where(reverse, turned[mirrored * height:(mirrored + 1) * height],
                              straight[c * height:(c + 1) * height])
            for level in range(levels):
                edge[level, number * species:(number + 1) * species, column(c)] = (
                    value[level * species:(level + 1) * species])

    zero_edge = jnp.zeros((8, width), jnp.float32)
    edge_rate[0] = zero_edge
    edge_upper[...] = zero_edge
    nothing = jnp.zeros((8, LANES), jnp.float32)

    def forward_edge(level, carry):
        previous = jnp.maximum(level - 1, 0)
        held, behind = None, nothing
        for c in range(chunks + 1):
            fresh = (None, nothing, nothing)
            if c < chunks:
                cols = column(c)
                south, north = edge_south[level, :, cols], edge_north[level, :, cols]
                moved = edge[level, :, cols]
                fresh = ((1.0 - south - north) * moved,
                         pltpu.roll(south * moved, LANES - 1, 1), pltpu.roll(north * moved, 1, 1))
            if c > 0:
                cols = column(c - 1)
                low, high = edge_rate[level, :, cols], edge_rate[level + 1, :, cols]
                inverse = 1.0 / ((1.0 + low + high) + low * edge_upper[:, cols])
                edge_upper[:, cols] = -high * inverse
                centre, left, right = held
                y_adjoint = (centre + jnp.where(lane_last[:8], fresh[1], left)
                             + jnp.where(lane_first[:8], behind, right))
                edge[level, :, cols] = (y_adjoint + low * edge[previous, :, cols]) * inverse
                behind = right
            held = fresh
        return carry

    lax.fori_loop(0, levels, forward_edge, 0)

    def out_copy(level):
        return pltpu.make_async_copy(solved.at[level], out_hbm.at[level], out_sem.at[level])

    def backward(step, carry):
        level = levels - 1 - step
        later = jnp.minimum(level + 1, levels - 1)
        for c in range(chunks):
            cols = column(c)
            factor = upper[level + 1, :, cols]
            for kind in range(species):
                value = solved[level, kind, :, cols]
                value = value + jnp.where(first, edge[level, kind:kind + 1, cols], 0.0)
                value = value + jnp.where(last, edge[level, species + kind:species + kind + 1, cols], 0.0)
                solved[level, kind, :, cols] = value - factor * solved[later, kind, :, cols]
        out_copy(level).start()
        return carry

    lax.fori_loop(0, levels, backward, 0)

    for c in range(chunks):
        for kind in range(species):
            flat[c, pl.ds(kind, rows, stride=8), :] = solved[0, kind, :, column(c)]
    regrid.wait()
    lane_parts = cells // LANES

    def regrid_row(row, carry):
        for part in range(per_row):
            surface = jnp.concatenate(
                [flat[part * lane_parts + p, pl.ds(pl.multiple_of(row * 8, 8), 8), :] for p in range(lane_parts)],
                axis=1).astype(jnp.bfloat16)
            block = row * per_row + part
            terms[pl.ds(pl.multiple_of(block * 8, 8), 8), :] = jnp.dot(
                surface, regrid_v[block], preferred_element_type=jnp.float32)
        return carry

    lax.fori_loop(0, rows, regrid_row, 0)
    target = owner_ref[...] * NI + slot_ref[...]
    select = lax.broadcasted_iota(jnp.int32, (count * NI, blocks), 0) == target
    select = select.astype(jnp.float32).astype(jnp.bfloat16)
    for kind in range(species):
        value = terms[pl.ds(kind, blocks, stride=8), :]
        total = sum(jnp.dot(select, piece, preferred_element_type=jnp.float32) for piece in pieces(value))
        for number in range(count):
            spot = (number % tiles % 2, number % tiles // 2, number // tiles, kind)
            part_ref[spot] = total[number * NI:(number + 1) * NI]

    order = list(range(1, chips)) + [0]
    first = {}
    for step in order:
        first[step] = pltpu.make_async_remote_copy(
            src_ref=part_ref.at[1 - core, chip_of[step]], dst_ref=in_a.at[step],
            send_sem=send_a.at[step], recv_sem=recv_a.at[step],
            device_id=partner, device_id_type=MESH)
        first[step].start()
    second = {}
    for step in order:
        first[step].wait_recv()
        sum_a[step] = part_ref[core, chip_of[step]] + in_a[step]
        if step > 0:
            second[step] = pltpu.make_async_remote_copy(
                src_ref=sum_a.at[step], dst_ref=in_b.at[step - 1],
                send_sem=send_b.at[step - 1], recv_sem=recv_b.at[step - 1],
                device_id=(face, 2 * chip_of[step] + core), device_id_type=MESH)
            second[step].start()
    for step in range(1, chips):
        second[step].wait_recv()
    total = sum_a[0]
    for step in range(1, chips):
        total = total + in_b[step - 1]
    sum_b[...] = total
    third = {}
    for step in range(1, faces):
        third[step] = pltpu.make_async_remote_copy(
            src_ref=sum_b.at[face_of[step]], dst_ref=in_c.at[step - 1],
            send_sem=send_c.at[step - 1], recv_sem=recv_c.at[step - 1],
            device_id=(face_of[step], tile), device_id_type=MESH)
        third[step].start()
    for step in range(1, faces):
        third[step].wait_recv()
    result = sum_b[face]
    for step in range(1, faces):
        result = result + in_c[step - 1]
    for kind in range(result.shape[0]):
        grad_ref[:, kind, :] = result[kind]
    for copies in (first, second, third):
        for copy in copies.values():
            copy.wait_send()
    for copy in exchange:
        copy.wait_send()
    for level in range(levels):
        out_copy(level).wait()


def per_device(faces, tiles, sensitivity, west_weight, east_weight, south_weight, north_weight,
               mixing_rate, extents, rotation, regrid_weight, owner, inv_slot):
    levels, species, rows, width = sensitivity.shape
    blocks, cells, inv_cells = regrid_weight.shape
    chips = tiles // 2
    f32 = jnp.float32
    hbm = pl.BlockSpec(memory_space=pltpu.HBM)
    vmem = pl.BlockSpec(memory_space=pltpu.VMEM)
    smem = pl.BlockSpec(memory_space=pltpu.SMEM)
    dma = pltpu.SemaphoreType.DMA
    unit = (species, NI, inv_cells)
    field, line, edge = (levels, rows, width), (levels * species, width), (levels, 2 * species, width)
    shapes = [sensitivity.shape] + [field] * 4 + [(levels + 1, rows, width)]
    scratch = [pltpu.VMEM(shape, f32) for shape in shapes]
    scratch += [pltpu.VMEM(regrid_weight.shape, regrid_weight.dtype)]
    shapes = [sensitivity.shape, (levels + 1, rows, width)] + [line] * 4 + [edge] * 3
    shapes += [(levels + 1, 2 * species, width), (2 * species, width)]
    shapes += [(width // LANES, rows * 8, LANES), (blocks * 8, inv_cells)]
    shapes += [(2, chips, faces) + unit, (chips, faces) + unit, (chips, faces) + unit]
    shapes += [(chips - 1, faces) + unit, (faces,) + unit, (faces - 1,) + unit]
    scratch += [pltpu.VMEM(shape, f32) for shape in shapes]
    scratch += [dma((5, levels)), dma, dma, dma((2,)), dma((2,)), dma((levels,))]
    scratch += [dma((number,)) for number in (chips, chips, chips - 1, chips - 1, faces - 1, faces - 1)]
    return pl.pallas_call(
        functools.partial(step_kernel, faces, tiles),
        out_shape=(
            jax.ShapeDtypeStruct(sensitivity.shape, f32),
            jax.ShapeDtypeStruct((NI, species, inv_cells), f32),
        ),
        in_specs=[smem, smem] + [hbm] * 7 + [vmem, vmem],
        out_specs=(hbm, vmem),
        scratch_shapes=scratch,
        compiler_params=pltpu.CompilerParams(
            collective_id=0, has_side_effects=True, vmem_limit_bytes=60 << 20),
        name="step",
    )(extents, rotation, sensitivity, west_weight, east_weight, south_weight, north_weight,
      mixing_rate, regrid_weight, owner.reshape(1, blocks), inv_slot.reshape(1, blocks))


def solution(mesh):
    faces, tiles = mesh.shape["face"], mesh.shape["tile"]
    both = ("face", "tile")
    placed = (P(None, None, both, None),) + (P(None, both, None),) * 5 + (P(), P()) + (
        P(both, None, None), P(both, None), P(both))
    return jax.shard_map(
        functools.partial(per_device, faces, tiles),
        mesh=mesh,
        in_specs=placed,
        out_specs=(P(None, None, both, None), P(both, None, None)),
        check_vma=False,
    )
```

```python
import functools

import jax
import jax.numpy as jnp
from jax import lax
from jax.experimental import pallas as pl
from jax.experimental.pallas import tpu as pltpu
from jax.sharding import PartitionSpec as P

NI = 8
LANES = 128
MESH = pl.DeviceIdType.MESH


def step_kernel(faces, tiles, ext_hbm, rot_hbm, sens_hbm, west_hbm, east_hbm, south_hbm, north_hbm,
                rate_hbm, regrid_hbm, owner_hbm, slot_hbm, solved, grad_ref,
                sens_v, west_v, east_v, south_v, north_v, rate_v, regrid_v, upper,
                east_edge, west_edge, from_west, from_east, edge, edge_south, edge_north, edge_rate, edge_upper,
                flat, terms, part_ref, in_a, sum_a, in_b, sum_b, in_c,
                ext_ref, rot_ref, owner_ref, slot_ref, small_sem, level_sem, rate_sem, regrid_sem, edge_send, edge_recv,
                send_a, recv_a, send_b, recv_b, send_c, recv_c):
    levels, species, rows, width = sens_v.shape
    chunks = width // LANES
    blocks, cells, inv_cells = regrid_v.shape
    per_row = width // cells
    face, tile = lax.axis_index("face"), lax.axis_index("tile")
    count, chips = faces * tiles, tiles // 2
    position = face * tiles + tile
    after, before = lax.rem(position + 1, count), lax.rem(position + count - 1, count)
    after = (after // tiles, lax.rem(after, tiles))
    before = (before // tiles, lax.rem(before, tiles))
    chip, core = tile // 2, lax.rem(tile, 2)
    partner = (face, tile + 1 - 2 * core)
    chip_of = [lax.rem(chip + step, chips) for step in range(chips)]
    face_of = [lax.rem(face + step, faces) for step in range(faces)]
    others = [after, before, partner]
    others += [(face, 2 * chip_of[step] + core) for step in range(1, chips)]
    others += [(face_of[step], tile) for step in range(1, faces)]
    barrier = pltpu.get_barrier_semaphore()
    for other in others:
        pl.semaphore_signal(barrier, inc=1, device_id=other, device_id_type=MESH)

    def level_copies(level, pairs, base):
        return [
            pltpu.make_async_copy(source.at[level], sink.at[level], level_sem.at[base + number, level])
            for number, (source, sink) in enumerate(pairs)
        ]

    x_pairs = ((sens_hbm, sens_v), (west_hbm, west_v), (east_hbm, east_v))
    y_pairs = ((south_hbm, south_v), (north_hbm, north_v))
    rates = pltpu.make_async_copy(rate_hbm, rate_v.at[pl.ds(1, levels - 1)], rate_sem)
    regrid = pltpu.make_async_copy(regrid_hbm, regrid_v, regrid_sem)
    small = [
        pltpu.make_async_copy(source, sink, small_sem.at[number])
        for number, (source, sink) in enumerate(
            ((ext_hbm, ext_ref), (rot_hbm, rot_ref), (owner_hbm, owner_ref), (slot_hbm, slot_ref)))
    ]
    for copy in small:
        copy.start()
    for level in range(levels):
        for copy in level_copies(level, x_pairs, 0):
            copy.start()
    rates.start()
    for level in range(levels):
        for copy in level_copies(level, y_pairs, 3):
            copy.start()
    regrid.start()

    for copy in small:
        copy.wait()
    extent = ext_ref[face, tile]
    row_ids = lax.broadcasted_iota(jnp.int32, (rows, LANES), 0)
    lane_ids = lax.broadcasted_iota(jnp.int32, (rows, LANES), 1)
    live = row_ids < extent
    first, last = row_ids == 0, row_ids == extent - 1
    bottom = row_ids == rows - 1
    lane_first, lane_last = lane_ids == 0, lane_ids == LANES - 1
    zero = jnp.zeros((rows, LANES), jnp.float32)
    zero_field = jnp.zeros((rows, width), jnp.float32)
    upper[0] = zero_field
    rate_v[0] = zero_field
    rate_v[levels] = zero_field
    for kind in range(species):
        solved[0, kind] = zero_field
    flat[...] = jnp.zeros_like(flat)

    def column(c):
        return slice(c * LANES, (c + 1) * LANES)

    for level in range(levels):
        for copy in level_copies(level, x_pairs, 0):
            copy.wait()
        for c in range(chunks):
            east_rows = jnp.where(last, east_v[level, :, column(c)], 0.0)
            for kind in range(species):
                row = level * species + kind
                east_edge[row:row + 1, column(c)] = jnp.sum(
                    east_rows * sens_v[level, kind, :, column(c)], axis=0, keepdims=True)
        west_row = west_v[level, 0:1, :]
        for kind in range(species):
            row = level * species + kind
            west_edge[row:row + 1, :] = west_row * sens_v[level, kind, 0:1, :]
    pl.semaphore_wait(barrier, len(others))
    exchange = [
        pltpu.make_async_remote_copy(
            src_ref=source, dst_ref=sink, send_sem=edge_send.at[number], recv_sem=edge_recv.at[number],
            device_id=other, device_id_type=MESH)
        for number, (source, sink, other) in enumerate(
            ((east_edge, from_west, after), (west_edge, from_east, before)))
    ]
    for copy in exchange:
        copy.start()

    rates.wait()
    half = lax.broadcasted_iota(jnp.int32, (8, LANES), 0) < species

    def edge_rows(value):
        tail = jnp.sum(jnp.where(last, value, 0.0), axis=0, keepdims=True)
        return jnp.where(half, jnp.broadcast_to(value[0:1], (8, LANES)), jnp.broadcast_to(tail, (8, LANES)))

    def forward(level, carry):
        for copy in level_copies(level, y_pairs, 3):
            copy.wait()
        previous = jnp.maximum(level - 1, 0)
        held = None
        behind = [zero] * species
        for c in range(chunks + 1):
            fresh = [(None, zero, zero)] * species
            if c < chunks:
                cols = column(c)
                west, east = west_v[level, :, cols], east_v[level, :, cols]
                south, north = south_v[level, :, cols], north_v[level, :, cols]
                edge_south[level, :, cols] = edge_rows(south)
                edge_north[level, :, cols] = edge_rows(north)
                keep_x = 1.0 - west - east
                keep_y = 1.0 - south - north
                fresh = []
                for kind in range(species):
                    adjoint = jnp.where(live, sens_v[level, kind, :, cols], 0.0)
                    up = jnp.where(bottom, 0.0, pltpu.roll(west * adjoint, rows - 1, 0))
                    down = jnp.where(first, 0.0, pltpu.roll(east * adjoint, 1, 0))
                    moved = jnp.where(live, keep_x * adjoint + up + down, 0.0)
                    fresh.append((
                        keep_y * moved,
                        pltpu.roll(south * moved, LANES - 1, 1),
                        pltpu.roll(north * moved, 1, 1),
                    ))
            if c > 0:
                cols = column(c - 1)
                low, high = rate_v[level, :, cols], rate_v[level + 1, :, cols]
                edge_rate[level + 1, :, cols] = edge_rows(high)
                pivot = (1.0 + low + high) + low * upper[level, :, cols]
                inverse = 1.0 / pivot
                upper[level + 1, :, cols] = -high * inverse
                for kind in range(species):
                    centre, left, right = held[kind]
                    y_adjoint = (centre + jnp.where(lane_last, fresh[kind][1], left)
                                 + jnp.where(lane_first, behind[kind], right))
                    solved[level, kind, :, cols] = (
                        y_adjoint + low * solved[previous, kind, :, cols]) * inverse
                behind = [held[kind][2] for kind in range(species)]
            held = fresh
        return carry

    lax.fori_loop(0, levels, forward, 0)

    after_rotation = rot_ref[after[0], after[1]]
    my_rotation = rot_ref[face, tile]
    back = (lax.broadcasted_iota(jnp.int32, (LANES, LANES), 0)
            + lax.broadcasted_iota(jnp.int32, (LANES, LANES), 1) == LANES - 1)
    back = back.astype(jnp.float32).astype(jnp.bfloat16)

    def pieces(value):
        high = value.astype(jnp.bfloat16)
        rest = value - high.astype(jnp.float32)
        middle = rest.astype(jnp.bfloat16)
        return high, middle, (rest - middle.astype(jnp.float32)).astype(jnp.bfloat16)

    for number, (source, rotation) in enumerate(((from_west, my_rotation), (from_east, after_rotation))):
        exchange[number].wait_recv()
        straight = jnp.concatenate([source[:, column(c)] for c in range(chunks)], axis=0)
        turned = sum(jnp.dot(piece, back, preferred_element_type=jnp.float32) for piece in pieces(straight))
        height = levels * species
        reverse = jnp.full((height, LANES), rotation, jnp.int32) == 1
        for c in range(chunks):
            mirrored = chunks - 1 - c
            value = jnp.where(reverse, turned[mirrored * height:(mirrored + 1) * height],
                              straight[c * height:(c + 1) * height])
            for level in range(levels):
                edge[level, number * species:(number + 1) * species, column(c)] = (
                    value[level * species:(level + 1) * species])

    zero_edge = jnp.zeros((8, width), jnp.float32)
    edge_rate[0] = zero_edge
    edge_upper[...] = zero_edge
    nothing = jnp.zeros((8, LANES), jnp.float32)

    def forward_edge(level, carry):
        previous = jnp.maximum(level - 1, 0)
        held, behind = None, nothing
        for c in range(chunks + 1):
            fresh = (None, nothing, nothing)
            if c < chunks:
                cols = column(c)
                south, north = edge_south[level, :, cols], edge_north[level, :, cols]
                moved = edge[level, :, cols]
                fresh = ((1.0 - south - north) * moved,
                         pltpu.roll(south * moved, LANES - 1, 1), pltpu.roll(north * moved, 1, 1))
            if c > 0:
                cols = column(c - 1)
                low, high = edge_rate[level, :, cols], edge_rate[level + 1, :, cols]
                inverse = 1.0 / ((1.0 + low + high) + low * edge_upper[:, cols])
                edge_upper[:, cols] = -high * inverse
                centre, left, right = held
                y_adjoint = (centre + jnp.where(lane_last[:8], fresh[1], left)
                             + jnp.where(lane_first[:8], behind, right))
                edge[level, :, cols] = (y_adjoint + low * edge[previous, :, cols]) * inverse
                behind = right
            held = fresh
        return carry

    lax.fori_loop(0, levels, forward_edge, 0)

    def backward(step, carry):
        level = levels - 1 - step
        later = jnp.minimum(level + 1, levels - 1)
        for c in range(chunks):
            cols = column(c)
            factor = upper[level + 1, :, cols]
            for kind in range(species):
                value = solved[level, kind, :, cols]
                value = value + jnp.where(first, edge[level, kind:kind + 1, cols], 0.0)
                value = value + jnp.where(last, edge[level, species + kind:species + kind + 1, cols], 0.0)
                solved[level, kind, :, cols] = value - factor * solved[later, kind, :, cols]
        return carry

    lax.fori_loop(0, levels, backward, 0)

    for c in range(chunks):
        for kind in range(species):
            flat[c, pl.ds(kind, rows, stride=8), :] = solved[0, kind, :, column(c)]
    regrid.wait()
    lane_parts = cells // LANES

    def regrid_row(row, carry):
        for part in range(per_row):
            surface = jnp.concatenate(
                [flat[part * lane_parts + p, pl.ds(pl.multiple_of(row * 8, 8), 8), :] for p in range(lane_parts)],
                axis=1).astype(jnp.bfloat16)
            block = row * per_row + part
            terms[pl.ds(pl.multiple_of(block * 8, 8), 8), :] = jnp.dot(
                surface, regrid_v[block], preferred_element_type=jnp.float32)
        return carry

    lax.fori_loop(0, rows, regrid_row, 0)
    target = owner_ref[...] * NI + slot_ref[...]
    select = lax.broadcasted_iota(jnp.int32, (count * NI, blocks), 0) == target
    select = select.astype(jnp.float32).astype(jnp.bfloat16)
    first = {}
    for kind in range(species):
        value = terms[pl.ds(kind, blocks, stride=8), :]
        total = sum(jnp.dot(select, piece, preferred_element_type=jnp.float32) for piece in pieces(value))
        for number in range(count):
            spot = (number % tiles % 2, kind, number % tiles // 2, number // tiles)
            part_ref[spot] = total[number * NI:(number + 1) * NI]
        first[kind] = pltpu.make_async_remote_copy(
            src_ref=part_ref.at[1 - core, kind], dst_ref=in_a.at[kind],
            send_sem=send_a.at[kind], recv_sem=recv_a.at[kind],
            device_id=partner, device_id_type=MESH)
        first[kind].start()

    order = list(range(1, chips)) + [0]
    for kind in range(species):
        first[kind].wait_recv()
    second = {}
    for step in order:
        for kind in range(species):
            sum_a[step, :, kind] = part_ref[core, kind, chip_of[step]] + in_a[kind, chip_of[step]]
        if step > 0:
            second[step] = pltpu.make_async_remote_copy(
                src_ref=sum_a.at[step], dst_ref=in_b.at[step - 1],
                send_sem=send_b.at[step - 1], recv_sem=recv_b.at[step - 1],
                device_id=(face, 2 * chip_of[step] + core), device_id_type=MESH)
            second[step].start()
    for step in range(1, chips):
        second[step].wait_recv()
    total = sum_a[0]
    for step in range(1, chips):
        total = total + in_b[step - 1]
    sum_b[...] = total
    third = {}
    for step in range(1, faces):
        third[step] = pltpu.make_async_remote_copy(
            src_ref=sum_b.at[face_of[step]], dst_ref=in_c.at[step - 1],
            send_sem=send_c.at[step - 1], recv_sem=recv_c.at[step - 1],
            device_id=(face_of[step], tile), device_id_type=MESH)
        third[step].start()
    for step in range(1, faces):
        third[step].wait_recv()
    result = sum_b[face]
    for step in range(1, faces):
        result = result + in_c[step - 1]
    for kind in range(result.shape[0]):
        grad_ref[:, kind, :] = result[kind]
    for copies in (first, second, third):
        for copy in copies.values():
            copy.wait_send()
    for copy in exchange:
        copy.wait_send()


def per_device(faces, tiles, sensitivity, west_weight, east_weight, south_weight, north_weight,
               mixing_rate, extents, rotation, regrid_weight, owner, inv_slot):
    levels, species, rows, width = sensitivity.shape
    blocks, cells, inv_cells = regrid_weight.shape
    chips = tiles // 2
    f32 = jnp.float32
    hbm = pl.BlockSpec(memory_space=pltpu.HBM)
    vmem = pl.BlockSpec(memory_space=pltpu.VMEM)
    dma = pltpu.SemaphoreType.DMA
    unit = (species, NI, inv_cells)
    field, line, edge = (levels, rows, width), (levels * species, width), (levels, 2 * species, width)
    shapes = [sensitivity.shape] + [field] * 4 + [(levels + 1, rows, width)]
    scratch = [pltpu.VMEM(shape, f32) for shape in shapes]
    scratch += [pltpu.VMEM(regrid_weight.shape, regrid_weight.dtype)]
    shapes = [(levels + 1, rows, width)] + [line] * 4 + [edge] * 3
    shapes += [(levels + 1, 2 * species, width), (2 * species, width)]
    shapes += [(width // LANES, rows * 8, LANES), (blocks * 8, inv_cells)]
    tail = (chips, faces, NI, inv_cells)
    shapes += [(2, species) + tail, (species,) + tail, (chips, faces) + unit]
    shapes += [(chips - 1, faces) + unit, (faces,) + unit, (faces - 1,) + unit]
    scratch += [pltpu.VMEM(shape, f32) for shape in shapes]
    scratch += [pltpu.SMEM(extents.shape, jnp.int32)] * 2 + [pltpu.VMEM((1, blocks), jnp.int32)] * 2
    scratch += [dma((4,)), dma((5, levels)), dma, dma, dma((2,)), dma((2,))]
    scratch += [dma((number,)) for number in (species, species, chips - 1, chips - 1, faces - 1, faces - 1)]
    pin = functools.partial(pltpu.with_memory_space_constraint, memory_space=pltpu.HBM)
    operands = (extents, rotation, sensitivity, west_weight, east_weight, south_weight, north_weight,
                mixing_rate, regrid_weight, owner.reshape(1, blocks), inv_slot.reshape(1, blocks))
    return pl.pallas_call(
        functools.partial(step_kernel, faces, tiles),
        out_shape=(
            jax.ShapeDtypeStruct(sensitivity.shape, f32),
            jax.ShapeDtypeStruct((NI, species, inv_cells), f32),
        ),
        in_specs=[hbm] * 11,
        out_specs=(vmem, vmem),
        scratch_shapes=scratch,
        compiler_params=pltpu.CompilerParams(
            collective_id=0, has_side_effects=True, vmem_limit_bytes=44 << 20),
        name="step",
    )(*[pin(operand) for operand in operands])


def solution(mesh):
    faces, tiles = mesh.shape["face"], mesh.shape["tile"]
    both = ("face", "tile")
    placed = (P(None, None, both, None),) + (P(None, both, None),) * 5 + (P(), P()) + (
        P(both, None, None), P(both, None), P(both))
    return jax.shard_map(
        functools.partial(per_device, faces, tiles),
        mesh=mesh,
        in_specs=placed,
        out_specs=(P(None, None, both, None), P(both, None, None)),
        check_vma=False,
    )
```
